512 devices in a mesh: row: 16 (over x, y_lo, core), col: 32 (over y_hi, z).
Axes of the slice: x: 4, y: 8 (y_hi: 4, y_lo: 2; y = y_hi * 2 + y_lo), z: 8, core: 2. Of those that a mesh axis runs over, the one named last changes fastest.
Arguments:
- features: float32 [65536, 256], P(('row', 'col')), may hold values from -6 to 6
- adj_tiles: bfloat16 [16, 32, 96, 128, 128], P('row', 'col'), may hold values from 0 to 1, as said below
- tile_dst: int32 [16, 32, 96], P('row', 'col'), may hold values from 0 to 15, as said below
- tile_src: int32 [16, 32, 96], P('row', 'col'), may hold values from 0 to 31, as said below
- tile_count: int32 [16, 32], P('row', 'col'), may hold values from 1 to 96, as said below
- self_weight: float32 [256, 256], replicated, may hold values from -0.375 to 0.375
- neighbor_weight: float32 [256, 256], replicated, may hold values from -1.5 to 1.5
- layer_bias: float32 [256], replicated, may hold values from -3 to 3
Outputs:
- activated: float32 [65536, 256], P(('row', 'col'))
The draws below stay inside these ranges and needn't reach their ends.
Inputs may be any that keep to these rules, and one draw needn't show every extreme that they name: `adj_tiles`: every entry is 0 or 1. `tile_dst`: a destination tile within the column group of the device. `tile_src`: a source tile within the row group of the device. `tile_count`: list entries at and beyond a device's count are padding; every device holds at least one listed tile; some device holds exactly 96.
All inputs are finite; a program needn't handle non-finite values.
Results may differ from the reference program's by a relative error of at most 0.0003.
Values sent between devices are 32-bit elements; how exact they have to be, the bound alone decides.
A program may use at most 64 MiB of HBM per device.

```python
import jax
import jax.numpy as jnp
from jax import lax

F = 256
F_OUT = 256
TILE = 128
NODE_DEV = 128
MAXT = 96
DST_TILES = 16
SRC_TILES = 32
NODES = 65536
N_ROW = 16
N_COL = 32


def draw_adj_tiles(key, part):
    linked = jax.random.bernoulli(key, 0.125, (N_ROW, N_COL, MAXT, TILE, TILE))
    return linked.astype(jnp.float32).astype(jnp.bfloat16)


def draw_tile_count(key, part):
    level = jax.random.randint(jax.random.fold_in(key, 1), (N_ROW, N_COL), 0, 4)
    jitter = jax.random.randint(jax.random.fold_in(key, 2), (N_ROW, N_COL), 0, MAXT // 8 + 1)
    counted = jnp.maximum(jnp.right_shift(jnp.int32(MAXT), level) - jitter, 1)
    chosen = jax.random.randint(jax.random.fold_in(key, 3), (), 0, N_ROW * N_COL)
    flat_counts = jnp.where(jnp.arange(N_ROW * N_COL) == chosen, MAXT, counted.reshape(-1))
    return flat_counts.reshape(N_ROW, N_COL).astype(jnp.int32)


def draw_tile_dst(key, part):
    raw_ids = jax.random.randint(jax.random.fold_in(key, 1), (N_ROW, N_COL, MAXT), 0, DST_TILES)
    isolated = jax.random.randint(jax.random.fold_in(key, 2), (N_COL,), 0, DST_TILES)
    flagged = jax.random.randint(jax.random.fold_in(key, 3), (N_COL,), 0, 2)
    struck = (raw_ids == isolated[None, :, None]) & (flagged[None, :, None] == 1)
    return jnp.where(struck, (raw_ids + 1) % DST_TILES, raw_ids).astype(jnp.int32)


def draw_tile_src(key, part):
    return jax.random.randint(key, (N_ROW, N_COL, MAXT), 0, SRC_TILES).astype(jnp.int32)


def level_of(own_key, shape, shards, low, top_value):
    gain, own = 1.0, jax.random.fold_in(own_key, 6)
    for position, parts in shards:
        draws = jnp.exp(jax.random.uniform(jax.random.fold_in(own, position), (parts,), jnp.float32, low / len(shards), top_value / len(shards)))
        gain = gain * jnp.repeat(draws, shape[position] // parts).reshape([-1 if axis == position else 1 for axis in range(len(shape))])
    return gain


def scatter_about(key, dims, width, reach, split=(), kind=jnp.bfloat16):
    entries = width * jax.random.normal(key, dims, jnp.float32)
    if split:
        entries = entries * level_of(key, dims, split, -0.22, 0.18)
    return jnp.clip(entries, -reach, reach).astype(kind)


def setup_inputs(seed: int = 0) -> dict:
    streams_of = jax.random.split(jax.random.key(seed), 9)
    features = scatter_about(streams_of[0], (NODES, F), 1.0, 6.0, ((0, 512),), jnp.float32)
    adj_tiles = draw_adj_tiles(jax.random.fold_in(streams_of[8], 71), 0)
    tile_dst = draw_tile_dst(jax.random.fold_in(streams_of[8], 71), 0)
    tile_src = draw_tile_src(jax.random.fold_in(streams_of[8], 71), 0)
    tile_count = draw_tile_count(jax.random.fold_in(streams_of[8], 71), 0)
    self_weight = scatter_about(streams_of[5], (F, F_OUT), F ** -0.5, 0.375, (), jnp.float32)
    neighbor_weight = scatter_about(streams_of[6], (F, F_OUT), 16 ** -0.5, 1.5, (), jnp.float32)
    layer_bias = scatter_about(streams_of[7], (F_OUT,), 0.5, 3.0, (), jnp.float32)
    return dict(features=features, adj_tiles=adj_tiles, tile_dst=tile_dst, tile_src=tile_src, tile_count=tile_count, self_weight=self_weight, neighbor_weight=neighbor_weight, layer_bias=layer_bias)


def reference(features, adj_tiles, tile_dst, tile_src, tile_count, self_weight, neighbor_weight, layer_bias):
    tiles_each = NODE_DEV // TILE
    tile_total = NODES // TILE
    devices_all = N_ROW * N_COL
    feature_tiles = features.reshape(tile_total, TILE, F)
    adjacency = adj_tiles.reshape(devices_all, MAXT, TILE, TILE)
    targets = tile_dst.reshape(devices_all, MAXT).astype(jnp.int32)
    sources = tile_src.reshape(devices_all, MAXT).astype(jnp.int32)
    counted = tile_count.reshape(devices_all).astype(jnp.int32)

    def visit(state_pair, entry):
        aggregate, degrees = state_pair
        device, blocks, target_ids, source_ids, valid_count = entry
        row_index = device // N_COL
        col_index = device % N_COL
        target_global = ((target_ids // tiles_each) * N_COL + col_index) * tiles_each + target_ids % tiles_each
        source_global = row_index * N_COL * tiles_each + source_ids
        live_slots = (jnp.arange(MAXT, dtype=jnp.int32) < valid_count).astype(jnp.float32)
        masked = blocks.astype(jnp.float32) * live_slots[:, None, None]
        products = jnp.einsum("kij,kjf->kif", masked, feature_tiles[source_global], precision=lax.Precision.HIGHEST)
        aggregate = aggregate.at[target_global].add(products)
        degrees = degrees.at[target_global].add(jnp.sum(masked, axis=2))
        return (aggregate, degrees), None

    start_pair = (jnp.zeros((tile_total, TILE, F), jnp.float32), jnp.zeros((tile_total, TILE), jnp.float32))
    (aggregate, degrees), _ = lax.scan(visit, start_pair, (jnp.arange(devices_all, dtype=jnp.int32), adjacency, targets, sources, counted))
    neighbor_mean = aggregate.reshape(NODES, F) / jnp.maximum(degrees.reshape(NODES), 1.0)[:, None]
    own_part = jnp.dot(features, self_weight, precision=lax.Precision.HIGHEST, preferred_element_type=jnp.float32)
    neighbor_part = jnp.dot(neighbor_mean, neighbor_weight, precision=lax.Precision.HIGHEST, preferred_element_type=jnp.float32)
    return jnp.maximum(own_part + neighbor_part + layer_bias, 0.0)
```

```python
import functools

import jax
import jax.numpy as jnp
from jax import lax
from jax.experimental import pallas as pl
from jax.experimental.pallas import tpu as pltpu
from jax.sharding import PartitionSpec as P

MESH = pl.DeviceIdType.MESH
NY, NZ = 4, 8
NX, NL, NC = 4, 2, 2
TILE, SLOTS, DSTS = 128, 96, 16
WIDE = 128
DEG = 8
SPLIT = 80
PARTS = ((0, SPLIT), (SPLIT, TILE - SPLIT))
PLUS, MINUS = 1, -1


def relays(chunk):
    found = []
    far = PLUS if chunk % 2 == 0 else MINUS
    base = {0: 0, 1: 1, 3: 1, 2: 2}
    for dy in (0, 3, 1, 2):
        sends = [(0, PLUS), (0, MINUS)]
        if dy == 0:
            sends = [(PLUS, 0), (MINUS, 0)] + sends
        if dy == 3 and far == PLUS:
            sends = [(PLUS, 0)] + sends
        if dy == 1 and far == MINUS:
            sends = [(MINUS, 0)] + sends
        found.append((base[dy], 0, 0, dy, 0, sends))
        up = 4 if dy in (0, 1) else 3
        for way, reach in ((PLUS, up), (MINUS, NZ - 1 - up)):
            for hop in range(1, reach + 1):
                sends = [(0, way)] if hop < reach else []
                found.append((base[dy] + hop, 1, 0, dy, (-way * hop) % NZ, sends))
    up = 4 if chunk % 2 == 0 else 3
    hops = [(0, 0, 0)]
    for way, reach in ((PLUS, up), (MINUS, NZ - 1 - up)):
        hops += [(way, hop, reach) for hop in range(1, reach + 1)]
    for way, hop, reach in hops:
        dz = (-way * hop) % NZ
        sends = [(PLUS, 0), (MINUS, 0)]
        if hop == 0:
            sends = [(0, PLUS), (0, MINUS)] + sends
        elif hop < reach:
            sends = [(0, way)] + sends
        found.append((hop, 0, 1, 0, dz, sends))
        out = PLUS if dz % 2 == 0 else MINUS
        found.append((hop + 1, 2, 1, 3, dz, [(PLUS, 0)] if out == PLUS else []))
        found.append((hop + 1, 2, 1, 1, dz, [(MINUS, 0)] if out == MINUS else []))
        found.append((hop + 2, 2, 1, 2, dz, []))
    rounds = [[] for _ in range(max(f[0] for f in found) + 1)]
    for f in sorted(found, key=lambda f: f[:2]):
        rounds[f[0]].append(f[2:])
    return rounds


def kernel(
    key_ref, cnt_ref, feat_ref, adj_hbm, ws_ref, wn_ref, bias_ref, out_ref,
    gath0, gath1, adj, cbuf, abuf, sbuf, got1, mine, got2, own,
    ssem, rsem, adj_sem, s1, q1, s2, q2,
):
    gath = (gath0, gath1)
    row, col = lax.axis_index("row"), lax.axis_index("col")
    y, z = col // NZ, lax.rem(col, NZ)
    x, lo, core = row // (NL * NC), lax.rem(row // NC, NL), lax.rem(row, NC)

    def col_at(dy, dz):
        return lax.rem(y + dy % NY, NY) * NZ + lax.rem(z + dz % NZ, NZ)

    def row_at(dx, dl):
        return (lax.rem(x + dx, NX) * NL + lax.rem(lo + dl, NL)) * NC + core

    sibling = row + 1 - 2 * core
    near = [(row, col_at(*e)) for e in ((1, 0), (-1, 0), (0, 1), (0, -1))]
    others = [(dx, dl) for dx in (2, 1, 3, 0) for dl in (1, 0) if (dx, dl) != (0, 0)]
    peers = near + [(sibling, col)] + [(row_at(*o), col) for o in others]

    fetch = pltpu.make_async_copy(adj_hbm, adj, adj_sem)
    fetch.start()
    for c in range(2):
        gath[c][col] = feat_ref[:, c * WIDE : (c + 1) * WIDE]

    barrier = pltpu.get_barrier_semaphore()
    for peer in peers:
        pl.semaphore_signal(barrier, inc=1, device_id=peer, device_id_type=MESH)
    pl.semaphore_wait(barrier, len(peers))

    started = []

    def piece(c, part, dy, dz, ey, ez, slot):
        first, size = PARTS[part]
        view = gath[c].at[col_at(dy, dz), pl.ds(first, size)]
        lands = ((c * 2 + part) * NY + (dy - ey) % NY) * NZ + (dz - ez) % NZ
        return pltpu.make_async_remote_copy(
            src_ref=view, dst_ref=view, send_sem=ssem.at[slot], recv_sem=rsem.at[lands],
            device_id=(row, col_at(ey, ez)), device_id_type=MESH,
        )

    plan = [relays(c) for c in range(2)]

    def relay(c, t):
        for part, dy, dz, sends in plan[c][t]:
            if not sends:
                continue
            if t:
                piece(c, part, dy, dz, 0, 0, 0).wait_recv()
            for ey, ez in sends:
                copy = piece(c, part, dy, dz, ey, ez, len(started))
                copy.start()
                started.append(copy)

    def arrive(c):
        for t, entries in enumerate(plan[c]):
            for part, dy, dz, sends in entries:
                if t and not sends:
                    piece(c, part, dy, dz, 0, 0, 0).wait_recv()

    def is_first(k):
        before = key_ref[jnp.maximum(k - 1, 0)]
        return (k == 0) | ((key_ref[k] >> 12) != (before >> 12))

    def degrees():
        fetch.wait()

        def add(k, acc):
            tile = adj[key_ref[k] & 127].astype(jnp.float32)
            acc = jnp.where(is_first(k), 0.0, acc) + tile
            abuf[k] = acc.astype(jnp.bfloat16)
            return acc

        lax.fori_loop(0, SLOTS, add, jnp.zeros((TILE, TILE), jnp.float32))
        ones = jnp.ones((DEG, TILE), jnp.bfloat16)

        def count(d, _):
            held, before = cnt_ref[d + 1], cnt_ref[d]
            tile = abuf[jnp.maximum(held - 1, 0)]
            deg = lax.dot_general(
                ones, tile, (((1,), (1,)), ((), ())), preferred_element_type=jnp.float32
            )
            sbuf[0, d // 2, lax.rem(d, 2), TILE:, :] = jnp.where(held > before, deg, 0.0)
            return 0

        lax.fori_loop(0, DSTS, count, 0)

    def own_part():
        own[...] = bias_ref[...] + jnp.dot(
            feat_ref[...], ws_ref[...], precision=lax.Precision.HIGHEST,
            preferred_element_type=jnp.float32,
        )

    def multiply(c, k0, k1, acc):
        def step(k, acc):
            key = key_ref[k]
            wide = gath[c][(key >> 7) & 31]
            high = wide.astype(jnp.bfloat16)
            low = (wide - high.astype(jnp.float32)).astype(jnp.bfloat16)
            both = jnp.concatenate([high, low], axis=1)
            prod = jnp.dot(adj[key & 127], both, preferred_element_type=jnp.float32)
            acc = jnp.where(is_first(k), 0.0, acc) + (prod[:, :WIDE] + prod[:, WIDE:])
            cbuf[k] = acc
            return acc

        return lax.fori_loop(k0, k1, step, acc, unroll=2)

    def rows_of(c):
        return TILE + (DEG if c == 0 else 0)

    def swap(c, half):
        return pltpu.make_async_remote_copy(
            src_ref=sbuf.at[c, pl.ds(half * 4, 4), 1 - core, pl.ds(0, rows_of(c))],
            dst_ref=got1.at[c, pl.ds(half * 4, 4), pl.ds(0, rows_of(c))],
            send_sem=s1.at[c * 2 + half], recv_sem=q1.at[c * 2 + half],
            device_id=(sibling, col), device_id_type=MESH,
        )

    def give(c, dx, dl):
        at = lax.rem(x + dx, NX) * NL + lax.rem(lo + dl, NL)
        n = dx * NL + dl
        return pltpu.make_async_remote_copy(
            src_ref=mine.at[c, at, pl.ds(0, rows_of(c))],
            dst_ref=got2.at[c, n, pl.ds(0, rows_of(c))],
            send_sem=s2.at[c * 8 + n], recv_sem=q2.at[c * 8 + n],
            device_id=(row_at(dx, dl), col), device_id_type=MESH,
        )

    def collect(c):
        def take(d, _):
            held, before = cnt_ref[d + 1], cnt_ref[d]
            tile = cbuf[jnp.maximum(held - 1, 0)]
            sbuf[c, d // 2, lax.rem(d, 2), :TILE, :] = jnp.where(held > before, tile, 0.0)
            return 0

        for half in range(2):
            lax.fori_loop(half * 8, half * 8 + 8, take, 0)
            swap(c, half).start()

    def spread(c):
        n = rows_of(c)
        for half in range(2):
            swap(c, half).wait_recv()
            for j in range(half * 4, half * 4 + 4):
                mine[c, j, :n] = sbuf[c, j, core, :n] + got1[c, j, :n]
        for dx, dl in others:
            give(c, dx, dl).start()

    def finish(c, scale):
        n = rows_of(c)
        total = mine[c, x * NL + lo, :n]
        for dx, dl in reversed(others):
            give(c, dx, dl).wait_recv()
            total = total + got2[c, dx * NL + dl, :n]
        if c == 0:
            deg = jnp.maximum(total[TILE : TILE + 1], 1.0)
            scale = jnp.broadcast_to(deg, (TILE, TILE)).T
        mean = total[:TILE] / scale
        own[...] += jnp.dot(
            mean, wn_ref[c * WIDE : (c + 1) * WIDE], precision=lax.Precision.HIGHEST,
            preferred_element_type=jnp.float32,
        )
        return scale

    zero = jnp.zeros((TILE, WIDE), jnp.float32)
    relay(0, 0)
    relay(1, 0)
    own_part()
    relay(0, 1)
    degrees()
    relay(0, 2)
    relay(1, 1)
    relay(0, 3)
    relay(1, 2)
    relay(0, 4)
    relay(0, 5)
    relay(0, 6)
    relay(1, 3)
    arrive(0)
    acc = multiply(0, 0, 32, zero)
    relay(1, 4)
    acc = multiply(0, 32, 64, acc)
    relay(1, 5)
    acc = multiply(0, 64, 96, acc)
    relay(1, 6)
    collect(0)
    spread(0)
    arrive(1)
    multiply(1, 0, 96, zero)
    collect(1)
    scale = finish(0, None)
    spread(1)
    finish(1, scale)
    out_ref[...] = jnp.maximum(own[...], 0.0)
    for copy in started:
        copy.wait_send()
    for c in range(2):
        for half in range(2):
            swap(c, half).wait_send()
        for dx, dl in others:
            give(c, dx, dl).wait_send()


def tables(dst, src, count):
    slot = jnp.arange(SLOTS, dtype=jnp.int32)
    key = jnp.where(slot < count, dst, DSTS) * 4096 + src * 128 + slot
    rank = jnp.sum((key[None, :] < key[:, None]).astype(jnp.int32), axis=1)
    spot = rank[:, None] == slot[None, :]
    ordered = jnp.sum(jnp.where(spot, key[:, None], 0), axis=0)
    place = jnp.arange(DSTS + 1, dtype=jnp.int32) * 4096
    counts = jnp.sum((key[:, None] < place[None, :]).astype(jnp.int32), axis=0)
    return ordered, counts


def on_device(features, adj_tiles, tile_dst, tile_src, tile_count, self_weight, neighbor_weight, layer_bias):
    ordered, counts = tables(tile_dst[0, 0], tile_src[0, 0], tile_count[0, 0])
    sends = sum(len(e[3]) for c in range(2) for r in relays(c) for e in r)
    smem = pl.BlockSpec(memory_space=pltpu.SMEM)
    vmem = pl.BlockSpec(memory_space=pltpu.VMEM)
    dma = pltpu.SemaphoreType.DMA
    f32, bf16 = jnp.float32, jnp.bfloat16
    return pl.pallas_call(
        kernel,
        out_shape=jax.ShapeDtypeStruct((TILE, 2 * WIDE), f32),
        in_specs=[smem, smem, vmem, pl.BlockSpec(memory_space=pl.ANY), vmem, vmem, vmem],
        out_specs=vmem,
        scratch_shapes=[
            pltpu.VMEM((NY * NZ, TILE, WIDE), f32),
            pltpu.VMEM((NY * NZ, TILE, WIDE), f32),
            pltpu.VMEM((SLOTS, TILE, TILE), bf16),
            pltpu.VMEM((SLOTS, TILE, WIDE), f32),
            pltpu.VMEM((SLOTS, TILE, TILE), bf16),
            pltpu.VMEM((2, NX * NL, NC, TILE + DEG, WIDE), f32),
            pltpu.VMEM((2, NX * NL, TILE + DEG, WIDE), f32),
            pltpu.VMEM((2, NX * NL, TILE + DEG, WIDE), f32),
            pltpu.VMEM((2, NX * NL, TILE + DEG, WIDE), f32),
            pltpu.VMEM((TILE, 2 * WIDE), f32),
            dma((sends,)), dma((4 * NY * NZ,)), dma,
            dma((4,)), dma((4,)), dma((16,)), dma((16,)),
        ],
        compiler_params=pltpu.CompilerParams(
            collective_id=0, has_side_effects=True, vmem_limit_bytes=48 * 1024 * 1024
        ),
        name="sage_layer",
    )(ordered, counts, features, adj_tiles[0, 0], self_weight, neighbor_weight, layer_bias[None])


def solution(mesh):
    placed = (
        P(("row", "col"), None),
        P("row", "col", None, None, None),
        P("row", "col", None),
        P("row", "col", None),
        P("row", "col"),
        P(),
        P(),
        P(),
    )
    return jax.shard_map(
        on_device, mesh=mesh, in_specs=placed, out_specs=P(("row", "col"), None), check_vma=False
    )
```

```python
import functools

import jax
import jax.numpy as jnp
from jax import lax
from jax.experimental import pallas as pl
from jax.experimental.pallas import tpu as pltpu
from jax.sharding import PartitionSpec as P

MESH = pl.DeviceIdType.MESH
NY, NZ = 4, 8
NX, NL, NC = 4, 2, 2
TILE, SLOTS, DSTS = 128, 96, 16
WIDE = 128
UNITS = ((0, 0, 128), (1, 0, 64), (1, 64, 64))
DEG = 8
SPLITS = (80, 88)
PLUS, MINUS = 1, -1


def relays(chunk):
    found = []
    far = PLUS if chunk % 2 == 0 else MINUS
    base = {0: 0, 1: 1, 3: 1, 2: 2}
    for dy in (0, 3, 1, 2):
        sends = [(0, PLUS), (0, MINUS)]
        if dy == 0:
            sends = [(PLUS, 0), (MINUS, 0)] + sends
        if dy == 3 and far == PLUS:
            sends = [(PLUS, 0)] + sends
        if dy == 1 and far == MINUS:
            sends = [(MINUS, 0)] + sends
        found.append((base[dy], 0, 0, dy, 0, sends))
        up = 4 if dy in (0, 1) else 3
        for way, reach in ((PLUS, up), (MINUS, NZ - 1 - up)):
            for hop in range(1, reach + 1):
                sends = [(0, way)] if hop < reach else []
                found.append((base[dy] + hop, 1, 0, dy, (-way * hop) % NZ, sends))
    up = 4 if chunk % 2 == 0 else 3
    hops = [(0, 0, 0)]
    for way, reach in ((PLUS, up), (MINUS, NZ - 1 - up)):
        hops += [(way, hop, reach) for hop in range(1, reach + 1)]
    for way, hop, reach in hops:
        dz = (-way * hop) % NZ
        sends = [(PLUS, 0), (MINUS, 0)]
        if hop == 0:
            sends = [(0, PLUS), (0, MINUS)] + sends
        elif hop < reach:
            sends = [(0, way)] + sends
        found.append((hop, 0, 1, 0, dz, sends))
        out = PLUS if dz % 2 == 0 else MINUS
        found.append((hop + 1, 2, 1, 3, dz, [(PLUS, 0)] if out == PLUS else []))
        found.append((hop + 1, 2, 1, 1, dz, [(MINUS, 0)] if out == MINUS else []))
        found.append((hop + 2, 2, 1, 2, dz, []))
    rounds = [[] for _ in range(max(f[0] for f in found) + 1)]
    for f in sorted(found, key=lambda f: f[:2]):
        rounds[f[0]].append(f[2:])
    return rounds


def kernel(
    feat_hbm, adj_hbm, dst_hbm, src_hbm, count_hbm, ws_hbm, wn_hbm, bias_hbm, out_ref,
    gath0, gath1, adj, cbuf, abuf, sbuf, got1, mine, got2, own,
    ws_ref, wn_ref, bias_ref, dst_ref, src_ref, count_ref, rows_ref, table,
    ssem, rsem, in_sem, s1, q1, s2, q2,
):
    gath = (gath0, gath1)
    row, col = lax.axis_index("row"), lax.axis_index("col")
    y, z = col // NZ, lax.rem(col, NZ)
    x, lo, core = row // (NL * NC), lax.rem(row // NC, NL), lax.rem(row, NC)

    def col_at(dy, dz):
        return lax.rem(y + dy % NY, NY) * NZ + lax.rem(z + dz % NZ, NZ)

    def row_at(dx, dl):
        return (lax.rem(x + dx, NX) * NL + lax.rem(lo + dl, NL)) * NC + core

    sibling = row + 1 - 2 * core
    near = [(row, col_at(*e)) for e in ((1, 0), (-1, 0), (0, 1), (0, -1))]
    others = [(dx, dl) for dx in (2, 1, 3, 0) for dl in (1, 0) if (dx, dl) != (0, 0)]
    peers = near + [(sibling, col)] + [(row_at(*o), col) for o in others]

    fetches = [
        pltpu.make_async_copy(src, dst, in_sem.at[n])
        for n, (src, dst) in enumerate((
            (feat_hbm.at[:, pl.ds(0, WIDE)], gath0.at[col]),
            (feat_hbm.at[:, pl.ds(WIDE, WIDE)], gath1.at[col]),
            (dst_hbm.at[0], dst_ref),
            (src_hbm.at[0], src_ref),
            (count_hbm, count_ref),
            (adj_hbm.at[0, 0], adj),
            (ws_hbm, ws_ref),
            (wn_hbm, wn_ref),
            (bias_hbm, bias_ref),
        ))
    ]
    for fetch in fetches:
        fetch.start()

    barrier = pltpu.get_barrier_semaphore()
    for peer in peers:
        pl.semaphore_signal(barrier, inc=1, device_id=peer, device_id_type=MESH)
    pl.semaphore_wait(barrier, len(peers))

    for fetch in fetches[:2]:
        fetch.wait()
    started = []

    def piece(c, part, dy, dz, ey, ez, slot):
        first, size = ((0, SPLITS[c]), (SPLITS[c], TILE - SPLITS[c]))[part]
        view = gath[c].at[col_at(dy, dz), pl.ds(first, size)]
        lands = ((c * 2 + part) * NY + (dy - ey) % NY) * NZ + (dz - ez) % NZ
        return pltpu.make_async_remote_copy(
            src_ref=view, dst_ref=view, send_sem=ssem.at[slot], recv_sem=rsem.at[lands],
            device_id=(row, col_at(ey, ez)), device_id_type=MESH,
        )

    plan = [relays(c) for c in range(2)]

    def relay(c, t):
        for part, dy, dz, sends in plan[c][t]:
            if not sends:
                continue
            if t:
                piece(c, part, dy, dz, 0, 0, 0).wait_recv()
            for ey, ez in sends:
                copy = piece(c, part, dy, dz, ey, ez, len(started))
                copy.start()
                started.append(copy)

    def arrive(c):
        for t, entries in enumerate(plan[c]):
            for part, dy, dz, sends in entries:
                if t and not sends:
                    piece(c, part, dy, dz, 0, 0, 0).wait_recv()

    def tables():
        for fetch in fetches[2:5]:
            fetch.wait()
        lane = lax.broadcasted_iota(jnp.int32, (1, SLOTS), 1)
        keys = jnp.where(lane < count_ref[0, 0], dst_ref[...], DSTS) * 4096
        keys = jnp.broadcast_to(keys + src_ref[...] * 128 + lane, (SLOTS, SLOTS))
        down = lax.broadcasted_iota(jnp.int32, (SLOTS, SLOTS), 0)
        across = lax.broadcasted_iota(jnp.int32, (SLOTS, SLOTS), 1)
        key = jnp.sum(jnp.where(down == across, keys, 0), axis=1, keepdims=True)
        rank = jnp.sum((keys < key).astype(jnp.int32), axis=1, keepdims=True)
        spread = jnp.where(rank == across, key, 0)
        rows_ref[0:1, 0:SLOTS] = jnp.sum(spread, axis=0, keepdims=True)
        below = (key < across * 4096).astype(jnp.int32)
        rows_ref[1:2, 0:SLOTS] = jnp.sum(below, axis=0, keepdims=True)
        copy = pltpu.make_async_copy(rows_ref, table, in_sem.at[9])
        copy.start()
        copy.wait()
        fetches[5].wait()

    def is_first(k):
        before = table[0, jnp.maximum(k - 1, 0)]
        return (k == 0) | ((table[0, k] >> 12) != (before >> 12))

    def sum_tiles(k0, k1, acc):
        def add(k, acc):
            tile = adj[table[0, k] & 127].astype(jnp.float32)
            acc = jnp.where(is_first(k), 0.0, acc) + tile
            abuf[k] = acc.astype(jnp.bfloat16)
            return acc

        return lax.fori_loop(k0, k1, add, acc, unroll=8)

    def degrees(d0, d1):
        ones = jnp.ones((DEG, TILE), jnp.bfloat16)

        def count(d, _):
            held, before = table[1, d + 1], table[1, d]
            tile = abuf[jnp.maximum(held - 1, 0)]
            deg = lax.dot_general(
                ones, tile, (((1,), (1,)), ((), ())), preferred_element_type=jnp.float32
            )
            sbuf[0, d // 2, lax.rem(d, 2), TILE:, :] = jnp.where(held > before, deg, 0.0)
            return 0

        lax.fori_loop(d0, d1, count, 0, unroll=8)

    def own_part():
        for fetch in fetches[6:]:
            fetch.wait()
        mine_in = jnp.concatenate([gath0[col], gath1[col]], axis=1)
        own[...] = bias_ref[...].reshape(1, 2 * WIDE) + jnp.dot(
            mine_in, ws_ref[...], precision=lax.Precision.HIGHEST,
            preferred_element_type=jnp.float32,
        )

    def multiply(u, k0, k1, acc):
        c, first, size = UNITS[u]

        def step(k, acc):
            key = table[0, k]
            wide = gath[c][(key >> 7) & 31]
            high = wide.astype(jnp.bfloat16)
            low = (wide - high.astype(jnp.float32)).astype(jnp.bfloat16)
            both = jnp.concatenate([high, low], axis=1)
            tile = adj[key & 127, first : first + size]
            prod = jnp.dot(tile, both, preferred_element_type=jnp.float32)
            acc = jnp.where(is_first(k), 0.0, acc) + (prod[:, :WIDE] + prod[:, WIDE:])
            cbuf[k, first : first + size] = acc
            return acc

        return lax.fori_loop(k0, k1, step, acc, unroll=16)

    def span(u):
        return UNITS[u][1], UNITS[u][2] + (DEG if u == 0 else 0)

    def swap(u, half):
        c, (first, n) = UNITS[u][0], span(u)
        return pltpu.make_async_remote_copy(
            src_ref=sbuf.at[c, pl.ds(half * 4, 4), 1 - core, pl.ds(first, n)],
            dst_ref=got1.at[c, pl.ds(half * 4, 4), pl.ds(first, n)],
            send_sem=s1.at[u * 2 + half], recv_sem=q1.at[u * 2 + half],
            device_id=(sibling, col), device_id_type=MESH,
        )

    def give(u, dx, dl):
        c, (first, n) = UNITS[u][0], span(u)
        at = lax.rem(x + dx, NX) * NL + lax.rem(lo + dl, NL)
        slot = dx * NL + dl
        return pltpu.make_async_remote_copy(
            src_ref=mine.at[c, at, pl.ds(first, n)],
            dst_ref=got2.at[c, slot, pl.ds(first, n)],
            send_sem=s2.at[u * 8 + slot], recv_sem=q2.at[u * 8 + slot],
            device_id=(row_at(dx, dl), col), device_id_type=MESH,
        )

    def collect(u):
        c, first, size = UNITS[u]

        def take(d, _):
            held, before = table[1, d + 1], table[1, d]
            tile = cbuf[jnp.maximum(held - 1, 0), first : first + size]
            tile = jnp.where(held > before, tile, 0.0)
            sbuf[c, d // 2, lax.rem(d, 2), first : first + size, :] = tile
            return 0

        for half in range(2):
            lax.fori_loop(half * 8, half * 8 + 8, take, 0)
            swap(u, half).start()

    def spread(u):
        c, (first, n) = UNITS[u][0], span(u)
        end = first + n
        for half in range(2):
            swap(u, half).wait_recv()
            for j in range(half * 4, half * 4 + 4):
                mine[c, j, first:end] = sbuf[c, j, core, first:end] + got1[c, j, first:end]
        for dx, dl in others:
            give(u, dx, dl).start()

    def finish(u, scale):
        c, (first, n) = UNITS[u][0], span(u)
        size, end = UNITS[u][2], first + n
        total = mine[c, x * NL + lo, first:end]
        for dx, dl in reversed(others):
            give(u, dx, dl).wait_recv()
            total = total + got2[c, dx * NL + dl, first:end]
        if u == 0:
            deg = jnp.maximum(total[TILE : TILE + 1], 1.0)
            scale = jnp.broadcast_to(deg, (TILE, TILE)).T
        mean = total[:size] / scale[first : first + size]
        own[first : first + size] += jnp.dot(
            mean, wn_ref[c * WIDE : (c + 1) * WIDE], precision=lax.Precision.HIGHEST,
            preferred_element_type=jnp.float32,
        )
        return scale

    zero = jnp.zeros((TILE, WIDE), jnp.float32)
    relay(0, 0)
    relay(1, 0)
    tables()
    relay(0, 1)
    relay(1, 1)
    own_part()
    relay(0, 2)
    acc = sum_tiles(0, 48, zero)
    relay(1, 2)
    sum_tiles(48, 96, acc)
    relay(0, 3)
    degrees(0, 8)
    relay(1, 3)
    degrees(8, 16)
    relay(0, 4)
    relay(0, 5)
    relay(1, 4)
    relay(0, 6)
    arrive(0)
    acc = multiply(0, 0, 48, zero)
    relay(1, 5)
    multiply(0, 48, 96, acc)
    relay(1, 6)
    collect(0)
    spread(0)
    part = jnp.zeros((UNITS[1][2], WIDE), jnp.float32)
    arrive(1)
    multiply(1, 0, 96, part)
    collect(1)
    acc = multiply(2, 0, 48, part)
    spread(1)
    multiply(2, 48, 96, acc)
    collect(2)
    scale = finish(0, None)
    spread(2)
    finish(1, scale)
    finish(2, scale)
    out_ref[...] = jnp.maximum(own[...], 0.0)
    for copy in started:
        copy.wait_send()
    for u in range(len(UNITS)):
        for half in range(2):
            swap(u, half).wait_send()
        for dx, dl in others:
            give(u, dx, dl).wait_send()


def on_device(features, adj_tiles, tile_dst, tile_src, tile_count, self_weight, neighbor_weight, layer_bias):
    sends = sum(len(e[3]) for c in range(2) for r in relays(c) for e in r)
    vmem = pl.BlockSpec(memory_space=pltpu.VMEM)
    dma = pltpu.SemaphoreType.DMA
    f32, bf16 = jnp.float32, jnp.bfloat16
    return pl.pallas_call(
        kernel,
        out_shape=jax.ShapeDtypeStruct((TILE, 2 * WIDE), f32),
        in_specs=[pl.BlockSpec(memory_space=pltpu.HBM)] * 8,
        out_specs=vmem,
        scratch_shapes=[
            pltpu.VMEM((NY * NZ, TILE, WIDE), f32),
            pltpu.VMEM((NY * NZ, TILE, WIDE), f32),
            pltpu.VMEM((SLOTS, TILE, TILE), bf16),
            pltpu.VMEM((SLOTS, TILE, WIDE), f32),
            pltpu.VMEM((SLOTS, TILE, TILE), bf16),
            pltpu.VMEM((2, NX * NL, NC, TILE + DEG, WIDE), f32),
            pltpu.VMEM((2, NX * NL, TILE + DEG, WIDE), f32),
            pltpu.VMEM((2, NX * NL, TILE + DEG, WIDE), f32),
            pltpu.VMEM((2, NX * NL, TILE + DEG, WIDE), f32),
            pltpu.VMEM((TILE, 2 * WIDE), f32),
            pltpu.VMEM((2 * WIDE, 2 * WIDE), f32),
            pltpu.VMEM((2 * WIDE, 2 * WIDE), f32),
            pltpu.VMEM((2 * WIDE,), f32),
            pltpu.VMEM((1, SLOTS), jnp.int32),
            pltpu.VMEM((1, SLOTS), jnp.int32),
            pltpu.SMEM((1, 1), jnp.int32),
            pltpu.VMEM((8, 128), jnp.int32),
            pltpu.SMEM((8, 128), jnp.int32),
            dma((sends,)), dma((4 * NY * NZ,)), dma((10,)),
            dma((6,)), dma((6,)), dma((24,)), dma((24,)),
        ],
        compiler_params=pltpu.CompilerParams(
            collective_id=0, has_side_effects=True, vmem_limit_bytes=56 * 1024 * 1024
        ),
        name="sage_layer",
    )(features, adj_tiles, tile_dst, tile_src, tile_count, self_weight, neighbor_weight, layer_bias)


def solution(mesh):
    placed = (
        P(("row", "col"), None),
        P("row", "col", None, None, None),
        P("row", "col", None),
        P("row", "col", None),
        P("row", "col"),
        P(),
        P(),
        P(),
    )
    return jax.shard_map(
        on_device, mesh=mesh, in_specs=placed, out_specs=P(("row", "col"), None), check_vma=False
    )
```

```python
import functools

import jax
import jax.numpy as jnp
from jax import lax
from jax.experimental import pallas as pl
from jax.experimental.pallas import tpu as pltpu
from jax.sharding import PartitionSpec as P

MESH = pl.DeviceIdType.MESH
NY, NZ = 4, 8
NX, NL, NC = 4, 2, 2
TILE, SLOTS, DSTS = 128, 96, 16
WIDE = 128
UNITS = ((0, 0, 128), (1, 0, 64), (1, 64, 64))
DEG = 8
SPLITS = (80, 88)
PLUS, MINUS = 1, -1


def relays(chunk):
    found = []
    far = PLUS if chunk % 2 == 0 else MINUS
    base = {0: 0, 1: 1, 3: 1, 2: 2}
    for dy in (0, 3, 1, 2):
        sends = [(0, PLUS), (0, MINUS)]
        if dy == 0:
            sends = [(PLUS, 0), (MINUS, 0)] + sends
        if dy == 3 and far == PLUS:
            sends = [(PLUS, 0)] + sends
        if dy == 1 and far == MINUS:
            sends = [(MINUS, 0)] + sends
        found.append((base[dy], 0, 0, dy, 0, sends))
        up = 4 if dy in (0, 1) else 3
        for way, reach in ((PLUS, up), (MINUS, NZ - 1 - up)):
            for hop in range(1, reach + 1):
                sends = [(0, way)] if hop < reach else []
                found.append((base[dy] + hop, 1, 0, dy, (-way * hop) % NZ, sends))
    up = 4 if chunk % 2 == 0 else 3
    hops = [(0, 0, 0)]
    for way, reach in ((PLUS, up), (MINUS, NZ - 1 - up)):
        hops += [(way, hop, reach) for hop in range(1, reach + 1)]
    for way, hop, reach in hops:
        dz = (-way * hop) % NZ
        sends = [(PLUS, 0), (MINUS, 0)]
        if hop == 0:
            sends = [(0, PLUS), (0, MINUS)] + sends
        elif hop < reach:
            sends = [(0, way)] + sends
        found.append((hop, 0, 1, 0, dz, sends))
        out = PLUS if dz % 2 == 0 else MINUS
        found.append((hop + 1, 2, 1, 3, dz, [(PLUS, 0)] if out == PLUS else []))
        found.append((hop + 1, 2, 1, 1, dz, [(MINUS, 0)] if out == MINUS else []))
        found.append((hop + 2, 2, 1, 2, dz, []))
    rounds = [[] for _ in range(max(f[0] for f in found) + 1)]
    for f in sorted(found, key=lambda f: f[:2]):
        rounds[f[0]].append(f[2:])
    return rounds


def kernel(
    feat_hbm, adj_hbm, dst_hbm, src_hbm, count_hbm, ws_hbm, wn_hbm, bias_hbm, out_ref,
    gath0, gath1, adj, cbuf, abuf, sbuf, got1, mine, got2, own,
    ws_ref, wn_ref, bias_ref, dst_ref, src_ref, count_ref, rows_ref, table, wide_ref,
    ssem, rsem, in_sem, s1, q1, s2, q2,
):
    gath = (gath0, gath1)
    row, col = lax.axis_index("row"), lax.axis_index("col")
    y, z = col // NZ, lax.rem(col, NZ)
    x, lo, core = row // (NL * NC), lax.rem(row // NC, NL), lax.rem(row, NC)

    def col_at(dy, dz):
        return lax.rem(y + dy % NY, NY) * NZ + lax.rem(z + dz % NZ, NZ)

    def row_at(dx, dl):
        return (lax.rem(x + dx, NX) * NL + lax.rem(lo + dl, NL)) * NC + core

    sibling = row + 1 - 2 * core
    near = [(row, col_at(*e)) for e in ((1, 0), (-1, 0), (0, 1), (0, -1))]
    others = [(dx, dl) for dx in (2, 1, 3, 0) for dl in (1, 0) if (dx, dl) != (0, 0)]
    peers = near + [(sibling, col)] + [(row_at(*o), col) for o in others]

    fetches = [
        pltpu.make_async_copy(src, dst, in_sem.at[n])
        for n, (src, dst) in enumerate((
            (feat_hbm.at[:, pl.ds(0, WIDE)], gath0.at[col]),
            (feat_hbm.at[:, pl.ds(WIDE, WIDE)], gath1.at[col]),
            (dst_hbm.at[0], dst_ref),
            (src_hbm.at[0], src_ref),
            (count_hbm, count_ref),
            (adj_hbm.at[0, 0], adj),
            (ws_hbm, ws_ref),
            (wn_hbm, wn_ref),
            (bias_hbm, bias_ref),
        ))
    ]
    barrier = pltpu.get_barrier_semaphore()
    for peer in peers:
        pl.semaphore_signal(barrier, inc=1, device_id=peer, device_id_type=MESH)
    for fetch in fetches:
        fetch.start()
    pl.semaphore_wait(barrier, len(peers))

    for fetch in fetches[:2]:
        fetch.wait()
    started = []

    def piece(c, part, dy, dz, ey, ez, slot):
        first, size = ((0, SPLITS[c]), (SPLITS[c], TILE - SPLITS[c]))[part]
        view = gath[c].at[col_at(dy, dz), pl.ds(first, size)]
        lands = ((c * 2 + part) * NY + (dy - ey) % NY) * NZ + (dz - ez) % NZ
        return pltpu.make_async_remote_copy(
            src_ref=view, dst_ref=view, send_sem=ssem.at[slot], recv_sem=rsem.at[lands],
            device_id=(row, col_at(ey, ez)), device_id_type=MESH,
        )

    plan = [relays(c) for c in range(2)]

    def relay(c, t):
        for part, dy, dz, sends in plan[c][t]:
            if not sends:
                continue
            if t:
                piece(c, part, dy, dz, 0, 0, 0).wait_recv()
            for ey, ez in sends:
                copy = piece(c, part, dy, dz, ey, ez, len(started))
                copy.start()
                started.append(copy)

    def arrive(c):
        for t, entries in enumerate(plan[c]):
            for part, dy, dz, sends in entries:
                if t and not sends:
                    piece(c, part, dy, dz, 0, 0, 0).wait_recv()

    def tables():
        for fetch in fetches[2:5]:
            fetch.wait()
        lane = lax.broadcasted_iota(jnp.int32, (1, SLOTS), 1)
        keys = jnp.where(lane < count_ref[0, 0], dst_ref[...], DSTS) * 4096
        keys = jnp.broadcast_to(keys + src_ref[...] * 128 + lane, (SLOTS, SLOTS))
        down = lax.broadcasted_iota(jnp.int32, (SLOTS, SLOTS), 0)
        across = lax.broadcasted_iota(jnp.int32, (SLOTS, SLOTS), 1)
        key = jnp.sum(jnp.where(down == across, keys, 0), axis=1, keepdims=True)
        rank = jnp.sum((keys < key).astype(jnp.int32), axis=1, keepdims=True)
        spread = jnp.where(rank == across, key, 0)
        rows_ref[0:1, 0:SLOTS] = jnp.sum(spread, axis=0, keepdims=True)
        below = (key < across * 4096).astype(jnp.int32)
        rows_ref[1:2, 0:SLOTS] = jnp.sum(below, axis=0, keepdims=True)
        copy = pltpu.make_async_copy(rows_ref, table, in_sem.at[9])
        copy.start()
        copy.wait()
        fetches[5].wait()

    def is_first(k):
        before = table[0, jnp.maximum(k - 1, 0)]
        return (k == 0) | ((table[0, k] >> 12) != (before >> 12))

    def sum_tiles(k0, k1, acc):
        def add(k, acc):
            tile = adj[table[0, k] & 127].astype(jnp.float32)
            acc = jnp.where(is_first(k), 0.0, acc) + tile
            abuf[k] = acc.astype(jnp.bfloat16)
            return acc

        return lax.fori_loop(k0, k1, add, acc, unroll=8)

    def degrees(d0, d1):
        ones = jnp.ones((DEG, TILE), jnp.bfloat16)

        def count(d, _):
            held, before = table[1, d + 1], table[1, d]
            tile = abuf[jnp.maximum(held - 1, 0)]
            deg = lax.dot_general(
                ones, tile, (((1,), (1,)), ((), ())), preferred_element_type=jnp.float32
            )
            sbuf[0, d // 2, lax.rem(d, 2), TILE:, :] = jnp.where(held > before, deg, 0.0)
            return 0

        lax.fori_loop(d0, d1, count, 0, unroll=8)

    def own_part():
        for fetch in fetches[6:]:
            fetch.wait()
        mine_in = jnp.concatenate([gath0[col], gath1[col]], axis=1)
        own[...] = bias_ref[...].reshape(1, 2 * WIDE) + jnp.dot(
            mine_in, ws_ref[...], precision=lax.Precision.HIGHEST,
            preferred_element_type=jnp.float32,
        )

    def both_parts(wide):
        high = wide.astype(jnp.bfloat16)
        low = (wide - high.astype(jnp.float32)).astype(jnp.bfloat16)
        return jnp.concatenate([high, low], axis=1)

    def split(c):
        def one(s, _):
            wide_ref[s] = both_parts(gath[c][s])
            return 0

        lax.fori_loop(0, NY * NZ, one, 0, unroll=4)

    def multiply(u, k0, k1, acc):
        c, first, size = UNITS[u]

        def step(k, acc):
            key = table[0, k]
            both = both_parts(gath[c][(key >> 7) & 31]) if u < 1 else wide_ref[(key >> 7) & 31]
            tile = adj[key & 127, first : first + size]
            prod = jnp.dot(tile, both, preferred_element_type=jnp.float32)
            acc = jnp.where(is_first(k), 0.0, acc) + (prod[:, :WIDE] + prod[:, WIDE:])
            cbuf[k, first : first + size] = acc
            return acc

        return lax.fori_loop(k0, k1, step, acc, unroll=16)

    def span(u):
        return UNITS[u][1], UNITS[u][2] + (DEG if u == 0 else 0)

    def swap(u, half):
        c, (first, n) = UNITS[u][0], span(u)
        return pltpu.make_async_remote_copy(
            src_ref=sbuf.at[c, pl.ds(half * 4, 4), 1 - core, pl.ds(first, n)],
            dst_ref=got1.at[c, pl.ds(half * 4, 4), pl.ds(first, n)],
            send_sem=s1.at[u * 2 + half], recv_sem=q1.at[u * 2 + half],
            device_id=(sibling, col), device_id_type=MESH,
        )

    def give(u, dx, dl):
        c, (first, n) = UNITS[u][0], span(u)
        at = lax.rem(x + dx, NX) * NL + lax.rem(lo + dl, NL)
        slot = dx * NL + dl
        return pltpu.make_async_remote_copy(
            src_ref=mine.at[c, at, pl.ds(first, n)],
            dst_ref=got2.at[c, slot, pl.ds(first, n)],
            send_sem=s2.at[u * 8 + slot], recv_sem=q2.at[u * 8 + slot],
            device_id=(row_at(dx, dl), col), device_id_type=MESH,
        )

    def collect(u):
        c, first, size = UNITS[u]

        def take(d, _):
            held, before = table[1, d + 1], table[1, d]
            tile = cbuf[jnp.maximum(held - 1, 0), first : first + size]
            tile = jnp.where(held > before, tile, 0.0)
            sbuf[c, d // 2, lax.rem(d, 2), first : first + size, :] = tile
            return 0

        for half in range(2):
            lax.fori_loop(half * 8, half * 8 + 8, take, 0)
            swap(u, half).start()

    def spread(u):
        c, (first, n) = UNITS[u][0], span(u)
        end = first + n
        for half in range(2):
            swap(u, half).wait_recv()
            for j in range(half * 4, half * 4 + 4):
                mine[c, j, first:end] = sbuf[c, j, core, first:end] + got1[c, j, first:end]
        for dx, dl in others:
            give(u, dx, dl).start()

    def finish(u, scale):
        c, (first, n) = UNITS[u][0], span(u)
        size, end = UNITS[u][2], first + n
        total = mine[c, x * NL + lo, first:end]
        for dx, dl in reversed(others):
            give(u, dx, dl).wait_recv()
            total = total + got2[c, dx * NL + dl, first:end]
        if u == 0:
            deg = jnp.maximum(total[TILE : TILE + 1], 1.0)
            scale = jnp.broadcast_to(deg, (TILE, TILE)).T
        mean = total[:size] / scale[first : first + size]
        own[first : first + size] += jnp.dot(
            mean, wn_ref[c * WIDE : (c + 1) * WIDE], precision=lax.Precision.HIGHEST,
            preferred_element_type=jnp.float32,
        )
        return scale

    def sent(u):
        for half in range(2):
            swap(u, half).wait_send()
        for dx, dl in others:
            give(u, dx, dl).wait_send()

    zero = jnp.zeros((TILE, WIDE), jnp.float32)
    relay(0, 0)
    relay(1, 0)
    relay(0, 1)
    relay(1, 1)
    relay(0, 2)
    tables()
    relay(1, 2)
    acc = sum_tiles(0, 48, zero)
    relay(0, 3)
    sum_tiles(48, 96, acc)
    relay(1, 3)
    own_part()
    relay(0, 4)
    degrees(0, 8)
    relay(0, 5)
    degrees(8, 16)
    relay(1, 4)
    arrive(0)
    acc = multiply(0, 0, 32, zero)
    relay(1, 5)
    multiply(0, 32, 96, acc)
    collect(0)
    spread(0)
    part = jnp.zeros((UNITS[1][2], WIDE), jnp.float32)
    arrive(1)
    split(1)
    multiply(1, 0, 96, part)
    collect(1)
    acc = multiply(2, 0, 48, part)
    spread(1)
    multiply(2, 48, 96, acc)
    collect(2)
    scale = finish(0, None)
    spread(2)
    for copy in started:
        copy.wait_send()
    sent(0)
    finish(1, scale)
    finish(2, scale)
    out_ref[...] = jnp.maximum(own[...], 0.0)
    sent(1)
    sent(2)


def on_device(features, adj_tiles, tile_dst, tile_src, tile_count, self_weight, neighbor_weight, layer_bias):
    sends = sum(len(e[3]) for c in range(2) for r in relays(c) for e in r)
    vmem = pl.BlockSpec(memory_space=pltpu.VMEM)
    dma = pltpu.SemaphoreType.DMA
    f32, bf16 = jnp.float32, jnp.bfloat16
    summed = pl.pallas_call(
        kernel,
        out_shape=jax.ShapeDtypeStruct((TILE, 2 * WIDE), f32),
        in_specs=[pl.BlockSpec(memory_space=pltpu.HBM)] * 8,
        out_specs=vmem,
        scratch_shapes=[
            pltpu.VMEM((NY * NZ, TILE, WIDE), f32),
            pltpu.VMEM((NY * NZ, TILE, WIDE), f32),
            pltpu.VMEM((SLOTS, TILE, TILE), bf16),
            pltpu.VMEM((SLOTS, TILE, WIDE), f32),
            pltpu.VMEM((SLOTS, TILE, TILE), bf16),
            pltpu.VMEM((2, NX * NL, NC, TILE + DEG, WIDE), f32),
            pltpu.VMEM((2, NX * NL, TILE + DEG, WIDE), f32),
            pltpu.VMEM((2, NX * NL, TILE + DEG, WIDE), f32),
            pltpu.VMEM((2, NX * NL, TILE + DEG, WIDE), f32),
            pltpu.VMEM((TILE, 2 * WIDE), f32),
            pltpu.VMEM((2 * WIDE, 2 * WIDE), f32),
            pltpu.VMEM((2 * WIDE, 2 * WIDE), f32),
            pltpu.VMEM((2 * WIDE,), f32),
            pltpu.VMEM((1, SLOTS), jnp.int32),
            pltpu.VMEM((1, SLOTS), jnp.int32),
            pltpu.SMEM((1, 1), jnp.int32),
            pltpu.VMEM((8, 128), jnp.int32),
            pltpu.SMEM((8, 128), jnp.int32),
            pltpu.VMEM((NY * NZ, TILE, 2 * WIDE), bf16),
            dma((sends,)), dma((4 * NY * NZ,)), dma((10,)),
            dma((6,)), dma((6,)), dma((24,)), dma((24,)),
        ],
        compiler_params=pltpu.CompilerParams(
            collective_id=0, has_side_effects=True, vmem_limit_bytes=56 * 1024 * 1024
        ),
        name="sage_layer",
    )(features, adj_tiles, tile_dst, tile_src, tile_count, self_weight, neighbor_weight, layer_bias)
    return summed


def solution(mesh):
    placed = (
        P(("row", "col"), None),
        P("row", "col", None, None, None),
        P("row", "col", None),
        P("row", "col", None),
        P("row", "col"),
        P(),
        P(),
        P(),
    )
    return jax.shard_map(
        on_device, mesh=mesh, in_specs=placed, out_specs=P(("row", "col"), None), check_vma=False
    )
```
